128 devices in a mesh: replica: 16 (over z_hi, x, core), shard: 8 (over z_lo, y).
Axes of the slice: x: 4, y: 4, z: 4 (z_hi: 2, z_lo: 2; z = z_hi * 2 + z_lo), core: 2. Of those that a mesh axis runs over, the one named last changes fastest.
Arguments:
- features: bfloat16 [32768, 8192], P(('replica', 'shard')), may hold values from -24 to 24
- key_grads: bfloat16 [32768, 1024], P(('replica', 'shard')), may hold values from -1.5 to 1.5
- key_weight: bfloat16 [8192, 1024], P('shard'), may hold values from -0.1875 to 0.1875
- momentum: float32 [16, 8192, 1024], P('replica', 'shard'), may hold values from -8 to 8
- worker_error: float32 [16, 8192, 1024], P('replica', 'shard'), may hold values from -2 to 2
- server_error: float32 [8, 1024, 1024], P('shard', 'replica'), may hold values from -2 to 2
Outputs:
- input_grads: bfloat16 [32768, 8192], P(('replica', 'shard'))
- synced_momentum: bfloat16 [8192, 1024], P('shard')
- new_worker_error: float32 [16, 8192, 1024], P('replica', 'shard')
- new_server_error: float32 [8, 1024, 1024], P('shard', 'replica')
The draws below stay inside these ranges and needn't reach their ends.
All inputs are finite; a program needn't handle non-finite values. Where the reference program divides by a largest or mean magnitude, that divisor is 1e-20 or more.
Results may differ from the reference program's by a relative error of at most 0.018.
Values may be sent and summed in bfloat16 or wider, within the bound.
No kernel may reach another device: no remote copies, remote signals or barrier semaphores. Data moves between devices by JAX's collectives and lax.ppermute only.
A program may use at most 128 MiB of HBM per device.

```python
import jax
import jax.numpy as jnp
from jax import lax

D = 8192
KVD = 1024
TOK_DEV = 256
REPLICAS = 16
ROWS = 32768
SHARD_ROWS = 1024
N_SHARD = 8


def draw_momentum(key, part):
    key_rows, key_cols, key_base = jax.random.split(key, 3)
    row_scale = jnp.exp(jax.random.uniform(key_rows, (REPLICAS, D, 1), minval=-1.2, maxval=1.2))
    col_scale = jnp.exp(jax.random.uniform(key_cols, (1, 1, KVD), minval=-0.6, maxval=0.6))
    base = jax.random.normal(key_base, (REPLICAS, D, KVD), dtype=jnp.float32)
    return jnp.clip(0.5 * base * row_scale * col_scale, -8.0, 8.0).astype(jnp.float32)


def spiked(array, stream_key, source, target, blocks, factor):
    def block_of(axis_at):
        return (jnp.arange(array.shape[axis_at]) // (array.shape[axis_at] // blocks)).reshape((-1,) + (1,) * (array.ndim - 1 - axis_at))

    one_side = jax.random.permutation(stream_key, blocks)[block_of(target)]
    other_side = (block_of(target) + blocks // 2) % blocks
    return jnp.where((block_of(source) == one_side) | (block_of(source) == other_side), factor * array, array)


def block_levels(key, dims, shards, low, high):
    level, own = 1.0, jax.random.fold_in(key, 6)
    for position, parts in shards:
        heights = jnp.exp(jax.random.uniform(jax.random.fold_in(own, position), (parts,), jnp.float32, low / len(shards), high / len(shards)))
        level = level * jnp.repeat(heights, dims[position] // parts).reshape([-1 if axis == position else 1 for axis in range(len(dims))])
    return level


def noise(stream_key, extent, deviation, reach, shards=(), kind=jnp.bfloat16):
    loudness = block_levels(stream_key, extent, shards, -0.22, 0.18) if shards else 1.0
    drawn = jax.random.normal(stream_key, extent, jnp.float32) * deviation * loudness
    return jnp.minimum(jnp.maximum(drawn, -reach), reach).astype(kind)


def heavy_noise(own_key, extent, spread, limit, cuts, heavy, held_as=jnp.bfloat16):
    result = spread * jax.random.normal(own_key, extent, jnp.float32)
    if cuts:
        result = result * block_levels(own_key, extent, cuts, -0.22, 0.18)
    return jnp.clip(spiked(result, jax.random.fold_in(own_key, 3), *heavy), -limit, limit).astype(held_as)


def setup_inputs(seed: int = 0) -> dict:
    keys = jax.random.split(jax.random.key(seed), 7)
    features = heavy_noise(keys[0], (ROWS, D), 1.0, 24.0, ((0, 128),), (0, 1, 128, 5.5))
    key_grads = noise(keys[1], (ROWS, KVD), 0.25, 1.5, ((0, 128),))
    key_weight = noise(keys[2], (D, KVD), KVD ** -0.5, 0.1875, ((0, 8),))
    momentum = draw_momentum(jax.random.fold_in(keys[6], 71), 0)
    worker_error = noise(keys[4], (REPLICAS, D, KVD), 0.3, 2.0, ((0, 16), (1, 8)), jnp.float32)
    server_error = noise(keys[5], (N_SHARD, SHARD_ROWS, KVD), 0.3, 2.0, ((0, 8), (1, 16)), jnp.float32)
    return dict(features=features, key_grads=key_grads, key_weight=key_weight, momentum=momentum, worker_error=worker_error, server_error=server_error)


decay_rate = 0.9


def compress(values):
    scale = jnp.mean(jnp.abs(values), axis=-1, keepdims=True) + 1e-6
    return (scale * jnp.tanh(values / scale)).astype(jnp.bfloat16)


def reference(features, key_grads, key_weight, momentum, worker_error, server_error):
    blocks = features.reshape(REPLICAS, N_SHARD, TOK_DEV, D)
    grad_blocks = key_grads.reshape(REPLICAS, N_SHARD, TOK_DEV, KVD)

    def replica_step(items):
        inputs, grads, moment, error = items

        def add_part(total, pair):
            part = jnp.dot(pair[0].T, pair[1], preferred_element_type=jnp.float32).astype(jnp.bfloat16)
            part = lax.optimization_barrier(part)
            return total + part.astype(jnp.float32), None

        weight_grad, _ = lax.scan(add_part, jnp.zeros((D, KVD), jnp.float32), (inputs, grads))
        flat = grads.reshape(N_SHARD * TOK_DEV, KVD)
        back = jnp.dot(flat, key_weight.T, preferred_element_type=jnp.float32).astype(jnp.bfloat16)
        value = decay_rate * moment + (1.0 - decay_rate) * weight_grad + error
        packed = compress(value)
        return back, value - packed.astype(jnp.float32), packed

    back, new_worker, packed = lax.map(replica_step, (blocks, grad_blocks, momentum, worker_error))
    held = jnp.sum(packed.astype(jnp.float32), axis=0) / REPLICAS + server_error.reshape(D, KVD)
    synced = compress(held)
    new_server = (held - synced.astype(jnp.float32)).reshape(N_SHARD, SHARD_ROWS, KVD)
    return back.reshape(ROWS, D), synced, new_worker, new_server
```

```python
import functools

import jax
import jax.numpy as jnp
from jax import lax
from jax.experimental import pallas as pl
from jax.experimental.pallas import tpu as pltpu
from jax.sharding import Mesh
from jax.sharding import PartitionSpec as P


decay_rate = 0.9
TOK = 256
BLK = 1024
KV = 1024
OWN = 64
SHARD = ("zl", "y")
CHIPS = ("zh", "x")
Z = ("zh", "core", "zl")


def compress(values):
    scale = jnp.mean(jnp.abs(values), axis=-1, keepdims=True) + 1e-06
    return (scale * jnp.tanh(values / scale)).astype(jnp.bfloat16)


def shift_y(step):
    return [(i, (i + step) % 4) for i in range(4)]


SWAP = [(0, 1), (1, 0)]


def shard_perm(dz, dy):
    return [(((z + dz) % 2) * 4 + (y + dy) % 4, z * 4 + y) for z in range(2) for y in range(4)]


def chip_perm(dh, dx):
    return [(((h + dh) % 2) * 4 + (x + dx) % 4, h * 4 + x) for h in range(2) for x in range(4)]


def z_perm():
    pairs = []
    for zh in range(2):
        for zl in range(2):
            z = zh * 2 + zl
            other = (z + 1) % 4 if z % 2 == 1 else (z + 3) % 4
            pairs.append(((zh * 2 + 0) * 2 + zl, (zh * 2 + 0) * 2 + (1 - zl)))
            pairs.append(((zh * 2 + 1) * 2 + zl, ((other // 2) * 2 + 1) * 2 + other % 2))
    return pairs


def grad_kernel(core_ref, *refs):
    feats = refs[:8]
    keys = refs[8:16]
    momentum, worker, new_worker, mine, other = refs[16:]
    acc = jnp.zeros(momentum.shape, jnp.float32)
    for f, k in zip(feats, keys):
        acc += lax.dot_general(
            f[...], k[...], (((0,), (0,)), ((), ())), preferred_element_type=jnp.float32
        )
    value = decay_rate * momentum[...] + (1.0 - decay_rate) * acc + worker[...]
    packed = compress(value)
    new_worker[...] = value - packed.astype(jnp.float32)
    groups = packed.reshape(-1, 2, OWN, KV)
    first = core_ref[0] == 0
    mine[...] = jnp.where(first, groups[:, 0], groups[:, 1])
    other[...] = jnp.where(first, groups[:, 1], groups[:, 0])


def grad_call(core, feats, keys, momentum, worker, rows=256):
    chunk = rows // (2 * OWN)
    feat_spec = pl.BlockSpec((TOK, rows), lambda i, c: (0, i))
    key_spec = pl.BlockSpec((TOK, KV), lambda i, c: (0, 0))
    row_spec = pl.BlockSpec((rows, KV), lambda i, c: (i, 0))
    half_spec = pl.BlockSpec((chunk, OWN, KV), lambda i, c: (i, 0, 0))
    half = jax.ShapeDtypeStruct((BLK // (2 * OWN), OWN, KV), jnp.bfloat16)
    return pl.pallas_call(
        grad_kernel,
        out_shape=(jax.ShapeDtypeStruct((BLK, KV), jnp.float32), half, half),
        grid_spec=pltpu.PrefetchScalarGridSpec(
            num_scalar_prefetch=1,
            grid=(BLK // rows,),
            in_specs=[feat_spec] * 8 + [key_spec] * 8 + [row_spec] * 2,
            out_specs=(row_spec, half_spec, half_spec),
        ),
        cost_estimate=pl.CostEstimate(
            flops=2 * 8 * TOK * BLK * KV, bytes_accessed=22 * 2**20, transcendentals=BLK * KV
        ),
    )(core, *feats, *keys, momentum, worker)


def per_device(features, key_grads, key_weight, momentum, worker_error, server_error):
    zl, y = lax.axis_index("zl"), lax.axis_index("y")
    zh, x = lax.axis_index("zh"), lax.axis_index("x")
    core = lax.axis_index("core")

    def columns(dz, dy):
        to = ((zl + dz) % 2) * 4 + (y + 4 - dy) % 4
        return lax.dynamic_slice_in_dim(features, to * BLK, BLK, axis=1)

    keys = {(0, 0): key_grads}
    keys[0, 3] = lax.ppermute(key_grads, "y", shift_y(1))
    keys[0, 1] = lax.ppermute(key_grads, "y", shift_y(-1))
    keys[1, 0] = lax.ppermute(key_grads, "zl", SWAP)
    half_weight = lax.dynamic_slice_in_dim(key_weight, core * (BLK // 2), BLK // 2, axis=0)
    got = lax.ppermute(half_weight, Z, z_perm())
    far_a = lax.ppermute(keys[0, 3][: TOK // 2], "y", shift_y(1))
    far_b = lax.ppermute(keys[0, 1][TOK // 2 :], "y", shift_y(-1))
    keys[1, 3] = lax.ppermute(keys[1, 0], "y", shift_y(1))
    keys[1, 1] = lax.ppermute(keys[1, 0], "y", shift_y(-1))
    keys[0, 2] = jnp.concatenate([far_a, far_b], axis=0)
    keys[1, 2] = lax.ppermute(keys[0, 2], "zl", SWAP)
    got_other = lax.ppermute(got, "core", SWAP)
    low = jnp.where(core == 0, got, got_other)
    high = jnp.where(core == 0, got_other, got)
    pair_weight = jnp.concatenate([low, high], axis=0)

    order = [(0, 0), (1, 0), (0, 1), (0, 3), (1, 1), (1, 3), (0, 2), (1, 2)]
    feats = {}
    for dz, dy in order:
        piece = columns(dz, dy)
        feats[dz, dy] = piece if (dz, dy) == (0, 0) else lax.ppermute(piece, SHARD, shard_perm(dz, dy))

    def back(block, weight):
        return lax.dot_general(
            block, weight, (((1,), (1,)), ((), ())), preferred_element_type=jnp.float32
        ).astype(jnp.bfloat16)

    input_grads = jnp.zeros((TOK, 8 * BLK), jnp.bfloat16)
    for dy in (0, 1, 3, 2):
        for dz, weight in ((0, key_weight), (1, pair_weight)):
            piece = back(keys[0, dy], weight)
            if dy:
                piece = lax.ppermute(piece, "y", shift_y(dy))
            at = ((zl + dz) % 2) * 4 + (y + 4 - dy) % 4
            input_grads = lax.dynamic_update_slice_in_dim(input_grads, piece, at * BLK, axis=1)

    new_worker, mine, other = grad_call(
        core.reshape(1).astype(jnp.int32),
        [feats[k] for k in order],
        [keys[k] for k in order],
        momentum[0],
        worker_error[0],
    )

    met = lax.ppermute(other, "core", SWAP)
    pair = (mine.astype(jnp.float32) + met.astype(jnp.float32)).astype(jnp.bfloat16)
    me = zh * 4 + x
    total = lax.dynamic_index_in_dim(pair, me, 0, keepdims=False).astype(jnp.float32)
    for dh, dx in [(0, 1), (0, 3), (1, 0), (1, 1), (1, 3), (0, 2), (1, 2)]:
        to = ((zh + dh) % 2) * 4 + (x + 4 - dx) % 4
        piece = lax.dynamic_index_in_dim(pair, to, 0, keepdims=False)
        total = total + lax.ppermute(piece, CHIPS, chip_perm(dh, dx)).astype(jnp.float32)
    held = total / 16 + server_error[0]
    block = compress(held)
    new_server = (held - block.astype(jnp.float32))[None]

    half = jnp.zeros((8, OWN, KV), jnp.bfloat16)
    for dh, dx in [(0, 0), (0, 1), (0, 3), (1, 0), (1, 1), (1, 3), (0, 2), (1, 2)]:
        piece = block if (dh, dx) == (0, 0) else lax.ppermute(block, CHIPS, chip_perm(dh, dx))
        at = ((zh + dh) % 2) * 4 + (x + dx) % 4
        half = lax.dynamic_update_index_in_dim(half, piece, at, 0)
    half_other = lax.ppermute(half, "core", SWAP)
    even = jnp.where(core == 0, half, half_other)
    odd = jnp.where(core == 0, half_other, half)
    synced = jnp.stack([even, odd], axis=1).reshape(BLK, KV)
    return input_grads, synced, new_worker[None], new_server


def solution(mesh):
    fine = Mesh(mesh.devices.reshape(2, 4, 2, 2, 4), ("zh", "x", "core", "zl", "y"))
    rep, shd = ("zh", "x", "core"), ("zl", "y")
    in_specs = (
        P(rep + shd, None),
        P(rep + shd, None),
        P(shd, None),
        P(rep, shd, None),
        P(rep, shd, None),
        P(shd, rep, None),
    )
    out_specs = (
        P(rep + shd, None),
        P(shd, None),
        P(rep, shd, None),
        P(shd, rep, None),
    )
    return jax.shard_map(
        per_device, mesh=fine, in_specs=in_specs, out_specs=out_specs, check_vma=False
    )
```

```python
import jax
import jax.numpy as jnp
from jax import lax
from jax.experimental import pallas as pl
from jax.experimental.pallas import tpu as pltpu
from jax.sharding import Mesh
from jax.sharding import PartitionSpec as P


decay_rate = 0.9
TOK = 256
BLK = 1024
KV = 1024
OWN = 64
SHARD = ("zl", "y")
CHIPS = ("zh", "x")
Z = ("zh", "core", "zl")
SWAP = [(0, 1), (1, 0)]


def compress(values):
    scale = jnp.mean(jnp.abs(values), axis=-1, keepdims=True) + 1e-06
    return (scale * jnp.tanh(values / scale)).astype(jnp.bfloat16)


def shift_y(step):
    return [(i, (i + step) % 4) for i in range(4)]


def shard_perm(dz, dy):
    return [(((z + dz) % 2) * 4 + (y + dy) % 4, z * 4 + y) for z in range(2) for y in range(4)]


def z_perm():
    pairs = []
    for zh in range(2):
        for zl in range(2):
            z = zh * 2 + zl
            other = (z + 1) % 4 if z % 2 == 1 else (z + 3) % 4
            pairs.append(((zh * 2 + 0) * 2 + zl, (zh * 2 + 0) * 2 + (1 - zl)))
            pairs.append(((zh * 2 + 1) * 2 + zl, ((other // 2) * 2 + 1) * 2 + other % 2))
    return pairs


def contract_tokens(feats, keys):
    acc = None
    for f, k in zip(feats, keys):
        part = lax.dot_general(
            f[...], k[...], (((0,), (0,)), ((), ())), preferred_element_type=jnp.float32
        )
        acc = part if acc is None else acc + part
    return acc


def first_kernel(f, k, momentum, worker, out):
    acc = contract_tokens([f], [k])
    out[...] = decay_rate * momentum[...] + (1.0 - decay_rate) * acc + worker[...]


def early_kernel(n, *refs):
    base, out = refs[2 * n :]
    out[...] = base[...] + (1.0 - decay_rate) * contract_tokens(refs[:n], refs[n : 2 * n])


def early_call(kernel, feats, keys, rest, rows=256):
    n = len(feats)
    feat_spec = pl.BlockSpec((TOK, rows), lambda i: (0, i))
    key_spec = pl.BlockSpec((TOK, KV), lambda i: (0, 0))
    row_spec = pl.BlockSpec((rows, KV), lambda i: (i, 0))
    return pl.pallas_call(
        kernel,
        out_shape=jax.ShapeDtypeStruct((BLK, KV), jnp.float32),
        grid=(BLK // rows,),
        in_specs=[feat_spec] * n + [key_spec] * n + [row_spec] * len(rest),
        out_specs=row_spec,
        cost_estimate=pl.CostEstimate(
            flops=2 * n * TOK * BLK * KV,
            bytes_accessed=(4 + 4 * len(rest) + n) * 2**20,
            transcendentals=0,
        ),
    )(*feats, *keys, *rest)


def late_kernel(feat_rows, key_rows, core_ref, *refs):
    n, m = len(feat_rows), len(key_rows)
    base, new_worker, mine, other = refs[n + m :]
    feats, keys = [], []
    at = 0
    for ref, size in zip(refs[n : n + m], key_rows):
        keys.append(ref)
        block, start = at // TOK, at % TOK
        feats.append(refs[block].at[pl.ds(start, size), :])
        at += size
    acc = contract_tokens(feats, keys)
    value = base[...] + (1.0 - decay_rate) * acc
    packed = compress(value)
    new_worker[...] = value - packed.astype(jnp.float32)
    groups = packed.reshape(-1, 2, OWN, KV)
    first = core_ref[0] == 0
    mine[...] = jnp.where(first, groups[:, 0], groups[:, 1])
    other[...] = jnp.where(first, groups[:, 1], groups[:, 0])


def late_call(core, feats, keys, base, rows=256):
    chunk = rows // (2 * OWN)
    feat_rows = [f.shape[0] for f in feats]
    key_rows = [k.shape[0] for k in keys]
    feat_spec = pl.BlockSpec((TOK, rows), lambda i, c: (0, i))
    key_specs = [pl.BlockSpec((r, KV), lambda i, c: (0, 0)) for r in key_rows]
    row_spec = pl.BlockSpec((rows, KV), lambda i, c: (i, 0))
    half_spec = pl.BlockSpec((chunk, OWN, KV), lambda i, c: (i, 0, 0))
    half = jax.ShapeDtypeStruct((BLK // (2 * OWN), OWN, KV), jnp.bfloat16)
    return pl.pallas_call(
        lambda *refs: late_kernel(feat_rows, key_rows, *refs),
        out_shape=(jax.ShapeDtypeStruct((BLK, KV), jnp.float32), half, half),
        grid_spec=pltpu.PrefetchScalarGridSpec(
            num_scalar_prefetch=1,
            grid=(BLK // rows,),
            in_specs=[feat_spec] * len(feats) + key_specs + [row_spec],
            out_specs=(row_spec, half_spec, half_spec),
        ),
        cost_estimate=pl.CostEstimate(
            flops=2 * sum(key_rows) * BLK * KV, bytes_accessed=14 * 2**20, transcendentals=BLK * KV
        ),
        name="late",
    )(core, *feats, *keys, base)


def back_kernel(core_ref, own, left, right, far_a, far_b, weight, got, got_other, *outs):
    j = pl.program_id(0)
    pair = jnp.where(core_ref[0] == j, got[...], got_other[...])

    def product(block, w):
        return lax.dot_general(
            block, w, (((1,), (1,)), ((), ())), preferred_element_type=jnp.float32
        ).astype(jnp.bfloat16)

    for dz, w in ((0, weight[...]), (1, pair)):
        for block, out in zip((own, left, right), outs[:3]):
            out[dz] = product(block[...], w)
        outs[3][dz, : TOK // 2] = product(far_a[...], w)
        outs[3][dz, TOK // 2 :] = product(far_b[...], w)


def back_call(core, blocks, weight, got, got_other):
    cols = BLK // 2

    def full(a):
        return pl.BlockSpec(a.shape, lambda j, c: (0, 0))

    out_spec = pl.BlockSpec((2, TOK, cols), lambda j, c: (0, 0, j))
    out = jax.ShapeDtypeStruct((2, TOK, BLK), jnp.bfloat16)
    return pl.pallas_call(
        back_kernel,
        out_shape=(out,) * 4,
        grid_spec=pltpu.PrefetchScalarGridSpec(
            num_scalar_prefetch=1,
            grid=(2,),
            in_specs=[full(b) for b in blocks]
            + [pl.BlockSpec((cols, KV), lambda j, c: (j, 0)), full(got), full(got_other)],
            out_specs=(out_spec,) * 4,
        ),
        cost_estimate=pl.CostEstimate(
            flops=2 * 4 * TOK * 2 * BLK * KV, bytes_accessed=10 * 2**20, transcendentals=0
        ),
        name="back",
    )(core, *blocks, weight, got, got_other)


def place_kernel(at_ref, *refs):
    pieces, out, buf, sem_in, sem_out = refs[:4], refs[4], refs[5], refs[6], refs[7]
    loads = [pltpu.make_async_copy(p, buf.at[i], sem_in.at[i]) for i, p in enumerate(pieces)]
    for load in loads:
        load.start()
    stores = []
    for i, load in enumerate(loads):
        load.wait()
        for dz in range(2):
            col = pl.multiple_of(at_ref[i, dz] * BLK, BLK)
            store = pltpu.make_async_copy(
                buf.at[i, dz], out.at[:, pl.ds(col, BLK)], sem_out.at[i, dz]
            )
            store.start()
            stores.append(store)
    for store in stores:
        store.wait()


def place_call(at, pieces):
    n = len(pieces)
    return pl.pallas_call(
        place_kernel,
        out_shape=jax.ShapeDtypeStruct((TOK, 8 * BLK), jnp.bfloat16),
        in_specs=[pl.BlockSpec(memory_space=pltpu.SMEM)] + [pl.BlockSpec(memory_space=pl.ANY)] * n,
        out_specs=pl.BlockSpec(memory_space=pl.ANY),
        scratch_shapes=[
            pltpu.VMEM((n, 2, TOK, BLK), jnp.bfloat16),
            pltpu.SemaphoreType.DMA((n,)),
            pltpu.SemaphoreType.DMA((n, 2)),
        ],
        cost_estimate=pl.CostEstimate(flops=0, bytes_accessed=8 * 2**20, transcendentals=0),
        name="place",
    )(at, *pieces)


def per_device(features, key_grads, key_weight, momentum, worker_error, server_error):
    zl, y = lax.axis_index("zl"), lax.axis_index("y")
    core = lax.axis_index("core")
    core_arg = core.reshape(1).astype(jnp.int32)
    fence = lax.optimization_barrier

    def columns(dz, dy):
        to = ((zl + dz) % 2) * 4 + (y + 4 - dy) % 4
        return lax.dynamic_slice_in_dim(features, to * BLK, BLK, axis=1)

    k10 = lax.ppermute(key_grads, "zl", SWAP)
    k03 = lax.ppermute(key_grads, "y", shift_y(1))
    k01 = lax.ppermute(key_grads, "y", shift_y(-1))
    half_weight = lax.dynamic_slice_in_dim(key_weight, core * (BLK // 2), BLK // 2, axis=0)
    order = [(0, 0), (1, 0), (0, 1), (0, 3), (1, 2), (1, 1), (1, 3), (0, 2)]
    pieces = {k: columns(*k) for k in order}
    flat = fence((k10, k03, k01, half_weight) + tuple(pieces.values()))
    k10, k03, k01, half_weight = flat[:4]
    pieces = dict(zip(order, flat[4:]))

    def send(key):
        return lax.ppermute(pieces[key], SHARD, shard_perm(*key))

    feats = {(0, 0): pieces[0, 0]}
    far_a = lax.ppermute(k03[: TOK // 2], "y", shift_y(1))
    far_b = lax.ppermute(k01[TOK // 2 :], "y", shift_y(-1))
    k13 = lax.ppermute(k10, "y", shift_y(1))
    k11 = lax.ppermute(k10, "y", shift_y(-1))
    got = lax.ppermute(half_weight, Z, z_perm())
    for key in order[1:5]:
        feats[key] = send(key)

    base = early_call(first_kernel, [feats[0, 0]], [key_grads], [momentum[0], worker_error[0]])

    flat = fence((far_a, far_b, k13, k11, got) + tuple(pieces[k] for k in order[5:]))
    far_a, far_b, k13, k11, got = flat[:5]
    pieces.update(zip(order[5:], flat[5:]))
    zfar_a = lax.ppermute(far_a, "zl", SWAP)
    zfar_b = lax.ppermute(far_b, "zl", SWAP)
    for key in order[5:]:
        feats[key] = send(key)

    got_other = lax.ppermute(got, "core", SWAP)
    early = [(1, 0), (0, 1), (0, 3)]
    early_keys = [k10, k01, k03]
    base = early_call(
        lambda *refs: early_kernel(len(early), *refs), [feats[k] for k in early], early_keys, [base]
    )
    backs = back_call(core_arg, (key_grads, k01, k03, far_a, far_b), key_weight, got, got_other)

    late = [(1, 1), (1, 3), (0, 2), (1, 2)]
    flat = fence(tuple(feats[k] for k in late) + (zfar_a, zfar_b, base) + tuple(backs))
    late_feats, (zfar_a, zfar_b, base), backs = flat[:4], flat[4:7], flat[7:]
    back_own, back_1, back_3, back_2 = backs
    home_1 = lax.ppermute(back_1, "y", shift_y(1))
    home_3 = lax.ppermute(back_3, "y", shift_y(-1))
    home_2 = lax.ppermute(back_2, "y", shift_y(2))
    new_worker, mine, other = late_call(
        core_arg, list(late_feats), [k11, k13, far_a, far_b, zfar_a, zfar_b], base
    )

    met = lax.ppermute(other, "core", SWAP)
    pair = (mine.astype(jnp.float32) + met.astype(jnp.float32)).astype(jnp.bfloat16)
    parts = lax.all_to_all(pair, CHIPS, 0, 0)
    held = jnp.sum(parts.astype(jnp.float32), axis=0) / 16 + server_error[0]
    block = compress(held)
    new_server = (held - block.astype(jnp.float32))[None]

    half = lax.all_to_all(jnp.broadcast_to(block[None], (8, OWN, KV)), CHIPS, 0, 0)
    half_other = lax.ppermute(half, "core", SWAP)
    is_mine = lax.broadcasted_iota(jnp.int32, (8, 2, OWN, KV), 1) == core
    synced = jnp.where(is_mine, half[:, None], half_other[:, None]).reshape(BLK, KV)

    dys = [0, 1, 3, 2]
    at = jnp.stack(
        [jnp.stack([((zl + dz) % 2) * 4 + (y + 4 - dy) % 4 for dz in range(2)]) for dy in dys]
    ).astype(jnp.int32)
    input_grads = place_call(at, [back_own, home_1, home_3, home_2])
    return input_grads, synced, new_worker[None], new_server


def solution(mesh):
    fine = Mesh(mesh.devices.reshape(2, 4, 2, 2, 4), ("zh", "x", "core", "zl", "y"))
    rep, shd = ("zh", "x", "core"), ("zl", "y")
    in_specs = (
        P(rep + shd, None),
        P(rep + shd, None),
        P(shd, None),
        P(rep, shd, None),
        P(rep, shd, None),
        P(shd, rep, None),
    )
    out_specs = (
        P(rep + shd, None),
        P(shd, None),
        P(rep, shd, None),
        P(shd, rep, None),
    )


    return jax.shard_map(
        per_device, mesh=fine, in_specs=in_specs, out_specs=out_specs, check_vma=False
    )
```

```python
import jax
import jax.numpy as jnp
from jax import lax
from jax.experimental import pallas as pl
from jax.experimental.pallas import tpu as pltpu
from jax.sharding import Mesh
from jax.sharding import PartitionSpec as P


decay_rate = 0.9
TOK = 256
BLK = 1024
KV = 1024
OWN = 64
SHARD = ("zl", "y")
CHIPS = ("zh", "x")
Z = ("zh", "zl")
SWAP = [(0, 1), (1, 0)]


def compress(values):
    scale = jnp.mean(jnp.abs(values), axis=-1, keepdims=True) + 1e-06
    return (scale * jnp.tanh(values / scale)).astype(jnp.bfloat16)


def shift_y(step):
    return [(i, (i + step) % 4) for i in range(4)]


def shard_perm(dz, dy):
    return [(((z + dz) % 2) * 4 + (y + dy) % 4, z * 4 + y) for z in range(2) for y in range(4)]


def z_perm():
    return [(z, (z + 1) % 4 if z % 2 else (z + 3) % 4) for z in range(4)]


def contract_tokens(feats, keys):
    acc = None
    for f, k in zip(feats, keys):
        part = lax.dot_general(
            f[...], k[...], (((0,), (0,)), ((), ())), preferred_element_type=jnp.float32
        )
        acc = part if acc is None else acc + part
    return acc


def first_kernel(f, k, momentum, worker, out):
    acc = contract_tokens([f], [k])
    out[...] = decay_rate * momentum[...] + (1.0 - decay_rate) * acc + worker[...]


def early_kernel(n, *refs):
    base, out = refs[2 * n :]
    out[...] = base[...] + (1.0 - decay_rate) * contract_tokens(refs[:n], refs[n : 2 * n])


def early_call(kernel, feats, keys, rest, rows=256):
    n = len(feats)
    feat_spec = pl.BlockSpec((TOK, rows), lambda i: (0, i))
    key_spec = pl.BlockSpec((TOK, KV), lambda i: (0, 0))
    row_spec = pl.BlockSpec((rows, KV), lambda i: (i, 0))
    return pl.pallas_call(
        kernel,
        out_shape=jax.ShapeDtypeStruct((BLK, KV), jnp.float32),
        grid=(BLK // rows,),
        in_specs=[feat_spec] * n + [key_spec] * n + [row_spec] * len(rest),
        out_specs=row_spec,
        cost_estimate=pl.CostEstimate(
            flops=2 * n * TOK * BLK * KV,
            bytes_accessed=(4 + 4 * len(rest) + n) * 2**20,
            transcendentals=0,
        ),
    )(*feats, *keys, *rest)


def late_kernel(feat_rows, key_rows, core_ref, *refs):
    n, m = len(feat_rows), len(key_rows)
    base, new_worker, mine, other = refs[n + m :]
    feats, keys = [], []
    at = 0
    for ref, size in zip(refs[n : n + m], key_rows):
        keys.append(ref)
        block, start = at // TOK, at % TOK
        feats.append(refs[block].at[pl.ds(start, size), :])
        at += size
    acc = contract_tokens(feats, keys)
    value = base[...] + (1.0 - decay_rate) * acc
    packed = compress(value)
    new_worker[...] = value - packed.astype(jnp.float32)
    groups = packed.reshape(-1, 2, OWN, KV)
    first = core_ref[0] == 0
    mine[...] = jnp.where(first, groups[:, 0], groups[:, 1])
    other[...] = jnp.where(first, groups[:, 1], groups[:, 0])


def late_call(core, feats, keys, base, rows=256):
    chunk = rows // (2 * OWN)
    feat_rows = [f.shape[0] for f in feats]
    key_rows = [k.shape[0] for k in keys]
    feat_spec = pl.BlockSpec((TOK, rows), lambda i, c: (0, i))
    key_specs = [pl.BlockSpec((r, KV), lambda i, c: (0, 0)) for r in key_rows]
    row_spec = pl.BlockSpec((rows, KV), lambda i, c: (i, 0))
    half_spec = pl.BlockSpec((chunk, OWN, KV), lambda i, c: (i, 0, 0))
    half = jax.ShapeDtypeStruct((BLK // (2 * OWN), OWN, KV), jnp.bfloat16)
    return pl.pallas_call(
        lambda *refs: late_kernel(feat_rows, key_rows, *refs),
        out_shape=(jax.ShapeDtypeStruct((BLK, KV), jnp.float32), half, half),
        grid_spec=pltpu.PrefetchScalarGridSpec(
            num_scalar_prefetch=1,
            grid=(BLK // rows,),
            in_specs=[feat_spec] * len(feats) + key_specs + [row_spec],
            out_specs=(row_spec, half_spec, half_spec),
        ),
        cost_estimate=pl.CostEstimate(
            flops=2 * sum(key_rows) * BLK * KV, bytes_accessed=14 * 2**20, transcendentals=BLK * KV
        ),
        name="late",
    )(core, *feats, *keys, base)


def back_kernel(core_ref, own, left, right, far_a, far_b, weight, got, got_other, *outs):
    j = pl.program_id(0)
    pair = jnp.where(core_ref[0] == j, got[...], got_other[...])

    def product(block, w):
        return lax.dot_general(
            block, w, (((1,), (1,)), ((), ())), preferred_element_type=jnp.float32
        ).astype(jnp.bfloat16)

    for dz, w in ((0, weight[...]), (1, pair)):
        for block, out in zip((own, left, right), outs[:3]):
            out[dz] = product(block[...], w)
        outs[3][dz, : TOK // 2] = product(far_a[...], w)
        outs[3][dz, TOK // 2 :] = product(far_b[...], w)


def back_call(core, blocks, weight, got, got_other):
    cols = BLK // 2

    def full(a):
        return pl.BlockSpec(a.shape, lambda j, c: (0, 0))

    out_spec = pl.BlockSpec((2, TOK, cols), lambda j, c: (0, 0, j))
    out = jax.ShapeDtypeStruct((2, TOK, BLK), jnp.bfloat16)
    return pl.pallas_call(
        back_kernel,
        out_shape=(out,) * 4,
        grid_spec=pltpu.PrefetchScalarGridSpec(
            num_scalar_prefetch=1,
            grid=(2,),
            in_specs=[full(b) for b in blocks]
            + [pl.BlockSpec((cols, KV), lambda j, c: (j, 0)), full(got), full(got_other)],
            out_specs=(out_spec,) * 4,
        ),
        cost_estimate=pl.CostEstimate(
            flops=2 * 4 * TOK * 2 * BLK * KV, bytes_accessed=10 * 2**20, transcendentals=0
        ),
        name="back",
    )(core, *blocks, weight, got, got_other)


def place_kernel(at_ref, *refs):
    pieces, out, buf, sem_in, sem_out = refs[:4], refs[4], refs[5], refs[6], refs[7]
    loads = [pltpu.make_async_copy(p, buf.at[i], sem_in.at[i]) for i, p in enumerate(pieces)]
    for load in loads:
        load.start()
    stores = []
    for i, load in enumerate(loads):
        load.wait()
        for dz in range(2):
            col = pl.multiple_of(at_ref[i, dz] * BLK, BLK)
            store = pltpu.make_async_copy(
                buf.at[i, dz], out.at[:, pl.ds(col, BLK)], sem_out.at[i, dz]
            )
            store.start()
            stores.append(store)
    for store in stores:
        store.wait()


def place_call(at, pieces):
    n = len(pieces)
    return pl.pallas_call(
        place_kernel,
        out_shape=jax.ShapeDtypeStruct((TOK, 8 * BLK), jnp.bfloat16),
        in_specs=[pl.BlockSpec(memory_space=pltpu.SMEM)] + [pl.BlockSpec(memory_space=pl.ANY)] * n,
        out_specs=pl.BlockSpec(memory_space=pl.ANY),
        scratch_shapes=[
            pltpu.VMEM((n, 2, TOK, BLK), jnp.bfloat16),
            pltpu.SemaphoreType.DMA((n,)),
            pltpu.SemaphoreType.DMA((n, 2)),
        ],
        cost_estimate=pl.CostEstimate(flops=0, bytes_accessed=8 * 2**20, transcendentals=0),
        name="place",
    )(at, *pieces)


def per_device(features, key_grads, key_weight, momentum, worker_error, server_error):
    zl, y = lax.axis_index("zl"), lax.axis_index("y")
    core = lax.axis_index("core")
    core_arg = core.reshape(1).astype(jnp.int32)
    fence = lax.optimization_barrier

    def columns(dz, dy):
        to = ((zl + dz) % 2) * 4 + (y + 4 - dy) % 4
        return lax.dynamic_slice_in_dim(features, to * BLK, BLK, axis=1)

    k10 = lax.ppermute(key_grads, "zl", SWAP)
    k03 = lax.ppermute(key_grads, "y", shift_y(1))
    k01 = lax.ppermute(key_grads, "y", shift_y(-1))
    half_weight = lax.dynamic_slice_in_dim(key_weight, core * (BLK // 2), BLK // 2, axis=0)
    got = lax.ppermute(half_weight, Z, z_perm())
    order = [(0, 0), (1, 0), (0, 1), (0, 3), (1, 2), (1, 1), (1, 3), (0, 2)]
    pieces = {k: columns(*k) for k in order}
    flat = fence((k10, k03, k01) + tuple(pieces.values()))
    k10, k03, k01 = flat[:3]
    pieces = dict(zip(order, flat[3:]))

    def send(key):
        return lax.ppermute(pieces[key], SHARD, shard_perm(*key))

    feats = {(0, 0): pieces[0, 0]}
    far_a = lax.ppermute(k03[: TOK // 2], "y", shift_y(1))
    far_b = lax.ppermute(k01[TOK // 2 :], "y", shift_y(-1))
    k13 = lax.ppermute(k10, "y", shift_y(1))
    k11 = lax.ppermute(k10, "y", shift_y(-1))
    for key in order[1:5]:
        feats[key] = send(key)

    base = early_call(first_kernel, [feats[0, 0]], [key_grads], [momentum[0], worker_error[0]])

    flat = fence((far_a, far_b, k13, k11, got) + tuple(pieces[k] for k in order[5:]))
    far_a, far_b, k13, k11, got = flat[:5]
    pieces.update(zip(order[5:], flat[5:]))
    zfar_a = lax.ppermute(far_a, "zl", SWAP)
    zfar_b = lax.ppermute(far_b, "zl", SWAP)
    for key in order[5:]:
        feats[key] = send(key)

    got_other = lax.ppermute(got, "core", SWAP)
    early = [(1, 0), (0, 1), (0, 3)]
    early_keys = [k10, k01, k03]
    base = early_call(
        lambda *refs: early_kernel(len(early), *refs), [feats[k] for k in early], early_keys, [base]
    )
    backs = back_call(core_arg, (key_grads, k01, k03, far_a, far_b), key_weight, got, got_other)

    late = [(1, 1), (1, 3), (0, 2), (1, 2)]
    flat = fence(tuple(feats[k] for k in late) + (zfar_a, zfar_b, base) + tuple(backs))
    late_feats, (zfar_a, zfar_b, base), backs = flat[:4], flat[4:7], flat[7:]
    back_own, back_1, back_3, back_2 = backs
    home_1 = lax.ppermute(back_1, "y", shift_y(1))
    home_3 = lax.ppermute(back_3, "y", shift_y(-1))
    home_2 = lax.ppermute(back_2, "y", shift_y(2))
    new_worker, mine, other = late_call(
        core_arg, list(late_feats), [k11, k13, far_a, far_b, zfar_a, zfar_b], base
    )

    met = lax.ppermute(other, "core", SWAP)
    pair = (mine.astype(jnp.float32) + met.astype(jnp.float32)).astype(jnp.bfloat16)
    parts = lax.all_to_all(pair, CHIPS, 0, 0)
    held = jnp.sum(parts.astype(jnp.float32), axis=0) / 16 + server_error[0]
    block = compress(held)
    new_server = (held - block.astype(jnp.float32))[None]

    half = lax.all_to_all(jnp.broadcast_to(block[None], (8, OWN, KV)), CHIPS, 0, 0)
    half_other = lax.ppermute(half, "core", SWAP)
    is_mine = lax.broadcasted_iota(jnp.int32, (8, 2, OWN, KV), 1) == core
    synced = jnp.where(is_mine, half[:, None], half_other[:, None]).reshape(BLK, KV)

    dys = [0, 1, 3, 2]
    at = jnp.stack(
        [jnp.stack([((zl + dz) % 2) * 4 + (y + 4 - dy) % 4 for dz in range(2)]) for dy in dys]
    ).astype(jnp.int32)
    input_grads = place_call(at, [back_own, home_1, home_3, home_2])
    return input_grads, synced, new_worker[None], new_server


def solution(mesh):
    fine = Mesh(mesh.devices.reshape(2, 4, 2, 2, 4), ("zh", "x", "core", "zl", "y"))
    rep, shd = ("zh", "x", "core"), ("zl", "y")
    in_specs = (
        P(rep + shd, None),
        P(rep + shd, None),
        P(shd, None),
        P(rep, shd, None),
        P(rep, shd, None),
        P(shd, rep, None),
    )
    out_specs = (
        P(rep + shd, None),
        P(shd, None),
        P(rep, shd, None),
        P(shd, rep, None),
    )


    return jax.shard_map(
        per_device, mesh=fine, in_specs=in_specs, out_specs=out_specs, check_vma=False
    )
```

```python
import jax
import jax.numpy as jnp
from jax import lax
from jax.experimental import pallas as pl
from jax.experimental.pallas import tpu as pltpu
from jax.sharding import Mesh
from jax.sharding import PartitionSpec as P


decay_rate = 0.9
TOK = 256
BLK = 1024
KV = 1024
OWN = 64
GRANT = 20 * 2**20
SHARD = ("zl", "y")
CHIPS = ("zh", "x")
Z = ("zh", "zl")
SWAP = [(0, 1), (1, 0)]


def compress(values):
    scale = jnp.mean(jnp.abs(values), axis=-1, keepdims=True) + 1e-06
    return (scale * jnp.tanh(values / scale)).astype(jnp.bfloat16)


def shift_y(step):
    return [(i, (i + step) % 4) for i in range(4)]


def shard_perm(dz, dy):
    return [(((z + dz) % 2) * 4 + (y + dy) % 4, z * 4 + y) for z in range(2) for y in range(4)]


def z_perm():
    return [(z, (z + 1) % 4 if z % 2 else (z + 3) % 4) for z in range(4)]


def contract_tokens(feats, keys):
    acc = None
    for f, k in zip(feats, keys):
        part = lax.dot_general(
            f[...], k[...], (((0,), (0,)), ((), ())), preferred_element_type=jnp.float32
        )
        acc = part if acc is None else acc + part
    return acc


def first_kernel(f, k, momentum, worker, out):
    acc = contract_tokens([f], [k])
    out[...] = decay_rate * momentum[...] + (1.0 - decay_rate) * acc + worker[...]


def early_kernel(n, *refs):
    base, out = refs[2 * n :]
    out[...] = base[...] + (1.0 - decay_rate) * contract_tokens(refs[:n], refs[n : 2 * n])


def early_call(kernel, feats, keys, rest, rows=256):
    n = len(feats)
    feat_spec = pl.BlockSpec((TOK, rows), lambda i: (0, i))
    key_spec = pl.BlockSpec((TOK, KV), lambda i: (0, 0))
    row_spec = pl.BlockSpec((rows, KV), lambda i: (i, 0))
    return pl.pallas_call(
        kernel,
        out_shape=jax.ShapeDtypeStruct((BLK, KV), jnp.float32),
        grid=(BLK // rows,),
        in_specs=[feat_spec] * n + [key_spec] * n + [row_spec] * len(rest),
        out_specs=row_spec,
        cost_estimate=pl.CostEstimate(
            flops=2 * n * TOK * BLK * KV,
            bytes_accessed=(4 + 4 * len(rest) + n) * 2**20,
            transcendentals=0,
        ),
        compiler_params=pltpu.CompilerParams(vmem_limit_bytes=GRANT),
    )(*feats, *keys, *rest)


def late_kernel(feat_rows, key_rows, core_ref, *refs):
    n, m = len(feat_rows), len(key_rows)
    base, new_worker, mine, other = refs[n + m :]
    feats, keys = [], []
    at = 0
    for ref, size in zip(refs[n : n + m], key_rows):
        keys.append(ref)
        block, start = at // TOK, at % TOK
        feats.append(refs[block].at[pl.ds(start, size), :])
        at += size
    acc = contract_tokens(feats, keys)
    value = base[...] + (1.0 - decay_rate) * acc
    packed = compress(value)
    new_worker[...] = value - packed.astype(jnp.float32)
    groups = packed.reshape(-1, 2, OWN, KV)
    first = core_ref[0] == 0
    mine[...] = jnp.where(first, groups[:, 0], groups[:, 1])
    other[...] = jnp.where(first, groups[:, 1], groups[:, 0])


def late_call(core, feats, keys, base, rows=256):
    chunk = rows // (2 * OWN)
    feat_rows = [f.shape[0] for f in feats]
    key_rows = [k.shape[0] for k in keys]
    feat_spec = pl.BlockSpec((TOK, rows), lambda i, c: (0, i))
    key_specs = [pl.BlockSpec((r, KV), lambda i, c: (0, 0)) for r in key_rows]
    row_spec = pl.BlockSpec((rows, KV), lambda i, c: (i, 0))
    half_spec = pl.BlockSpec((chunk, OWN, KV), lambda i, c: (i, 0, 0))
    half = jax.ShapeDtypeStruct((BLK // (2 * OWN), OWN, KV), jnp.bfloat16)
    return pl.pallas_call(
        lambda *refs: late_kernel(feat_rows, key_rows, *refs),
        out_shape=(jax.ShapeDtypeStruct((BLK, KV), jnp.float32), half, half),
        grid_spec=pltpu.PrefetchScalarGridSpec(
            num_scalar_prefetch=1,
            grid=(BLK // rows,),
            in_specs=[feat_spec] * len(feats) + key_specs + [row_spec],
            out_specs=(row_spec, half_spec, half_spec),
        ),
        cost_estimate=pl.CostEstimate(
            flops=2 * sum(key_rows) * BLK * KV, bytes_accessed=14 * 2**20, transcendentals=BLK * KV
        ),
        compiler_params=pltpu.CompilerParams(vmem_limit_bytes=GRANT),
        name="late",
    )(core, *feats, *keys, base)


def back_kernel(core_ref, own, left, right, far_a, far_b, weight, got, got_other, *outs):
    j = pl.program_id(0)
    pair = jnp.where(core_ref[0] == j, got[...], got_other[...])

    def product(block, w):
        return lax.dot_general(
            block, w, (((1,), (1,)), ((), ())), preferred_element_type=jnp.float32
        ).astype(jnp.bfloat16)

    for dz, w in ((0, weight[...]), (1, pair)):
        for block, out in zip((own, left, right), outs[:3]):
            out[dz] = product(block[...], w)
        outs[3][dz, : TOK // 2] = product(far_a[...], w)
        outs[3][dz, TOK // 2 :] = product(far_b[...], w)


def back_call(core, blocks, weight, got, got_other):
    cols = BLK // 2

    def full(a):
        return pl.BlockSpec(a.shape, lambda j, c: (0, 0))

    out_spec = pl.BlockSpec((2, TOK, cols), lambda j, c: (0, 0, j))
    out = jax.ShapeDtypeStruct((2, TOK, BLK), jnp.bfloat16)
    return pl.pallas_call(
        back_kernel,
        out_shape=(out,) * 4,
        grid_spec=pltpu.PrefetchScalarGridSpec(
            num_scalar_prefetch=1,
            grid=(2,),
            in_specs=[full(b) for b in blocks]
            + [pl.BlockSpec((cols, KV), lambda j, c: (j, 0)), full(got), full(got_other)],
            out_specs=(out_spec,) * 4,
        ),
        cost_estimate=pl.CostEstimate(
            flops=2 * 4 * TOK * 2 * BLK * KV, bytes_accessed=10 * 2**20, transcendentals=0
        ),
        compiler_params=pltpu.CompilerParams(vmem_limit_bytes=GRANT),
        name="back",
    )(core, *blocks, weight, got, got_other)


def place_kernel(at_ref, *refs):
    pieces, out, buf, sem_in, sem_out = refs[:4], refs[4], refs[5], refs[6], refs[7]
    loads = [pltpu.make_async_copy(p, buf.at[i], sem_in.at[i]) for i, p in enumerate(pieces)]
    for load in loads:
        load.start()
    stores = []
    for i, load in enumerate(loads):
        load.wait()
        for dz in range(2):
            col = pl.multiple_of(at_ref[i, dz] * BLK, BLK)
            store = pltpu.make_async_copy(
                buf.at[i, dz], out.at[:, pl.ds(col, BLK)], sem_out.at[i, dz]
            )
            store.start()
            stores.append(store)
    for store in stores:
        store.wait()


def place_call(at, pieces):
    n = len(pieces)
    return pl.pallas_call(
        place_kernel,
        out_shape=jax.ShapeDtypeStruct((TOK, 8 * BLK), jnp.bfloat16),
        in_specs=[pl.BlockSpec(memory_space=pltpu.SMEM)] + [pl.BlockSpec(memory_space=pl.ANY)] * n,
        out_specs=pl.BlockSpec(memory_space=pl.ANY),
        scratch_shapes=[
            pltpu.VMEM((n, 2, TOK, BLK), jnp.bfloat16),
            pltpu.SemaphoreType.DMA((n,)),
            pltpu.SemaphoreType.DMA((n, 2)),
        ],
        cost_estimate=pl.CostEstimate(flops=0, bytes_accessed=8 * 2**20, transcendentals=0),
        compiler_params=pltpu.CompilerParams(vmem_limit_bytes=GRANT),
        name="place",
    )(at, *pieces)


def per_device(features, key_grads, key_weight, momentum, worker_error, server_error):
    zl, y = lax.axis_index("zl"), lax.axis_index("y")
    core = lax.axis_index("core")
    core_arg = core.reshape(1).astype(jnp.int32)
    fence = lax.optimization_barrier

    def columns(dz, dy):
        to = ((zl + dz) % 2) * 4 + (y + 4 - dy) % 4
        return lax.dynamic_slice_in_dim(features, to * BLK, BLK, axis=1)

    k10 = lax.ppermute(key_grads, "zl", SWAP)
    k03 = lax.ppermute(key_grads, "y", shift_y(1))
    k01 = lax.ppermute(key_grads, "y", shift_y(-1))
    half_weight = lax.dynamic_slice_in_dim(key_weight, core * (BLK // 2), BLK // 2, axis=0)
    got = lax.ppermute(half_weight, Z, z_perm())
    order = [(0, 0), (1, 0), (1, 1), (1, 3), (1, 2), (0, 1), (0, 3), (0, 2)]
    pieces = {k: columns(*k) for k in order}
    flat = fence((k10, k03, k01) + tuple(pieces.values()))
    k10, k03, k01 = flat[:3]
    pieces = dict(zip(order, flat[3:]))

    def send(key):
        return lax.ppermute(pieces[key], SHARD, shard_perm(*key))

    feats = {(0, 0): pieces[0, 0]}
    far_a = lax.ppermute(k03[: TOK // 2], "y", shift_y(1))
    far_b = lax.ppermute(k01[TOK // 2 :], "y", shift_y(-1))
    k13 = lax.ppermute(k10, "y", shift_y(1))
    k11 = lax.ppermute(k10, "y", shift_y(-1))
    for key in order[1:5]:
        feats[key] = send(key)

    base = early_call(first_kernel, [feats[0, 0]], [key_grads], [momentum[0], worker_error[0]])

    flat = fence((far_a, far_b, got) + tuple(pieces[k] for k in order[5:]))
    far_a, far_b, got = flat[:3]
    pieces.update(zip(order[5:], flat[3:]))
    zfar_a = lax.ppermute(far_a, "zl", SWAP)
    zfar_b = lax.ppermute(far_b, "zl", SWAP)
    for key in order[5:]:
        feats[key] = send(key)

    got_other = lax.ppermute(got, "core", SWAP)
    early = [(1, 0), (1, 1), (1, 3)]
    early_keys = [k10, k11, k13]
    base = early_call(
        lambda *refs: early_kernel(len(early), *refs), [feats[k] for k in early], early_keys, [base]
    )
    backs = back_call(core_arg, (key_grads, k01, k03, far_a, far_b), key_weight, got, got_other)

    late = [(0, 1), (0, 3), (0, 2), (1, 2)]
    flat = fence(tuple(feats[k] for k in late) + (zfar_a, zfar_b, base) + tuple(backs))
    late_feats, (zfar_a, zfar_b, base), backs = flat[:4], flat[4:7], flat[7:]
    back_own, back_1, back_3, back_2 = backs
    home_1 = lax.ppermute(back_1, "y", shift_y(1))
    home_3 = lax.ppermute(back_3, "y", shift_y(-1))
    home_2 = lax.ppermute(back_2, "y", shift_y(2))
    new_worker, mine, other = late_call(
        core_arg, list(late_feats), [k01, k03, far_a, far_b, zfar_a, zfar_b], base
    )

    met = lax.ppermute(other, "core", SWAP)
    pair = (mine.astype(jnp.float32) + met.astype(jnp.float32)).astype(jnp.bfloat16)
    parts = lax.all_to_all(pair, CHIPS, 0, 0)
    held = jnp.sum(parts.astype(jnp.float32), axis=0) / 16 + server_error[0]
    block = compress(held)
    new_server = (held - block.astype(jnp.float32))[None]

    half = lax.all_to_all(jnp.broadcast_to(block[None], (8, OWN, KV)), CHIPS, 0, 0)
    half_other = lax.ppermute(half, "core", SWAP)
    is_mine = lax.broadcasted_iota(jnp.int32, (8, 2, OWN, KV), 1) == core
    synced = jnp.where(is_mine, half[:, None], half_other[:, None]).reshape(BLK, KV)

    dys = [0, 1, 3, 2]
    at = jnp.stack(
        [jnp.stack([((zl + dz) % 2) * 4 + (y + 4 - dy) % 4 for dz in range(2)]) for dy in dys]
    ).astype(jnp.int32)
    input_grads = place_call(at, [back_own, home_1, home_3, home_2])
    return input_grads, synced, new_worker[None], new_server


def solution(mesh):
    fine = Mesh(mesh.devices.reshape(2, 4, 2, 2, 4), ("zh", "x", "core", "zl", "y"))
    rep, shd = ("zh", "x", "core"), ("zl", "y")
    in_specs = (
        P(rep + shd, None),
        P(rep + shd, None),
        P(shd, None),
        P(rep, shd, None),
        P(rep, shd, None),
        P(shd, rep, None),
    )
    out_specs = (
        P(rep + shd, None),
        P(shd, None),
        P(rep, shd, None),
        P(shd, rep, None),
    )


    return jax.shard_map(
        per_device, mesh=fine, in_specs=in_specs, out_specs=out_specs, check_vma=False
    )
```
